32 devices in a mesh: pts: 16 (over z, x, core), proto: 2 (over y).
Axes of the slice: x: 2, y: 2, z: 4, core: 2. Of those that a mesh axis runs over, the one named last changes fastest.
Arguments:
- points: bfloat16 [128, 128, 1024], P('pts', None, 'proto'), as said below
- prototypes: bfloat16 [32, 512, 1024], P(('pts', 'proto')), as said below
- coarse_duals: float32 [32, 512], P(('pts', 'proto')), may hold values from -8 to 8
- active: int32 [128, 8], P('pts'), may hold values from 0 to 31, as said below
Outputs:
- point_duals: float32 [128, 128], P('pts')
- new_duals: float32 [32, 512], P(('pts', 'proto'))
The draws below stay inside these ranges and needn't reach their ends.
Inputs may be any that keep to these rules, and one draw needn't show every extreme that they name: `active`: each row names 8 different blocks. Block b belongs to owner group b // 2. The 8 rows of one index of pts name any one owner group at most 8 times, and exactly that often for 8 groups. Over all rows every owner group is named 64 times in all, every block at least once and at most 32 times, and in every owner group some block exactly 32 times. `points`: Real-valued embeddings. `prototypes`: Real-valued embeddings.
All inputs are finite; a program needn't handle non-finite values.
Results may differ from the reference program's by a relative error of at most 0.0003.
Values may be sent and summed in bfloat16 or wider, within the bound.
A program may use at most 128 MiB of HBM per device.

```python
import math
import jax
import jax.numpy as jnp
from jax import lax

D = 1024
BLOCK_ROWS = 128
BLOCK_COLS = 512
ACTIVE = 8
POINT_BLOCKS = 8
GROUP_CAP = 8
REACH = 8
BLOCK_MOST = 32
ALL_POINT_BLOCKS = 128
PROTO_BLOCKS = 32
N_PTS = 16
N_PROTO = 2


def pair_plan(key):
    groups = N_PTS
    owners = N_PROTO
    pair_total = POINT_BLOCKS * ACTIVE
    base = jax.random.fold_in(key, 7001)
    key_offset, key_sigma, key_perm, key_heavy, key_random = jax.random.split(base, 5)
    offsets = jax.random.permutation(key_offset, groups)[:REACH].astype(jnp.int32)
    sigma = jax.vmap(lambda k: jax.random.permutation(k, REACH))(jax.random.split(key_sigma, groups)).astype(jnp.int32)
    pair_ids = jnp.arange(pair_total, dtype=jnp.int32)
    copy_index = pair_ids // REACH
    chosen = sigma[:, pair_ids % REACH]
    source = jnp.arange(groups, dtype=jnp.int32)[:, None]
    dest = (source + offsets[chosen]) % groups
    arrival = chosen * GROUP_CAP + copy_index[None, :]
    perms = jax.vmap(lambda k: jax.random.permutation(k, pair_total))(jax.random.split(key_perm, groups)).astype(jnp.int32)
    heavy = jax.random.randint(key_heavy, (groups,), 0, owners).astype(jnp.int32)
    spread = (pair_total - BLOCK_MOST) // 6
    places = jnp.arange(pair_total, dtype=jnp.int32)
    random_local = jax.random.randint(key_random, (groups, pair_total), 0, owners - 1).astype(jnp.int32)
    cycle_local = (places - BLOCK_MOST - spread) % (owners - 1)
    other = jnp.where(places[None, :] < BLOCK_MOST + spread, random_local, cycle_local[None, :])
    load_map = jnp.where(places[None, :] < BLOCK_MOST, heavy[:, None], (heavy[:, None] + 1 + other) % owners)
    placed = perms[dest, arrival]
    local = load_map[dest, placed]
    chosen_blocks = dest * owners + local
    return chosen_blocks.reshape(groups * POINT_BLOCKS, ACTIVE).astype(jnp.int32)


def proto_values(key):
    base = jax.random.fold_in(key, 7002)
    key_value, key_scale = jax.random.split(base)
    normal = jnp.clip(jax.random.normal(key_value, (PROTO_BLOCKS, BLOCK_COLS, D), jnp.float32), -5.0, 5.0)
    scale = jnp.exp(jax.random.uniform(key_scale, (PROTO_BLOCKS, BLOCK_COLS, 1), jnp.float32, math.log(0.3), math.log(3.0)))
    return normal * scale * D ** (-0.5)


def draw_active(key, part):
    return pair_plan(key)


def draw_prototypes(key, part):
    return proto_values(key).astype(jnp.bfloat16)


def draw_points(key, part):
    base = jax.random.fold_in(key, 7003)
    key_value, key_scale = jax.random.split(base)
    normal = jnp.clip(jax.random.normal(key_value, (ALL_POINT_BLOCKS, BLOCK_ROWS, D), jnp.float32), -5.0, 5.0)
    scale = jnp.exp(jax.random.uniform(key_scale, (ALL_POINT_BLOCKS, BLOCK_ROWS, 1), jnp.float32, math.log(0.3), math.log(3.0)))
    values = normal * scale
    return values.astype(jnp.bfloat16)


def block_levels(stream_key, dims, cuts, least, high):
    level, own = 1.0, jax.random.fold_in(stream_key, 6)
    for axis_at, blocks in cuts:
        draws = jnp.exp(jax.random.uniform(jax.random.fold_in(own, axis_at), (blocks,), jnp.float32, least / len(cuts), high / len(cuts)))
        level = level * jnp.repeat(draws, dims[axis_at] // blocks).reshape([-1 if axis == axis_at else 1 for axis in range(len(dims))])
    return level


def bell_draw(stream_key, extent, scale, most, shards=(), kind=jnp.bfloat16):
    loudness = block_levels(stream_key, extent, shards, -0.22, 0.18) if shards else 1.0
    values = jax.random.normal(stream_key, extent, jnp.float32) * scale * loudness
    return jnp.minimum(jnp.maximum(values, -most), most).astype(kind)


def setup_inputs(seed: int = 0) -> dict:
    streams_of = jax.random.split(jax.random.key(seed), 5)
    return {
        "points": draw_points(jax.random.fold_in(streams_of[4], 71), 0),
        "prototypes": draw_prototypes(jax.random.fold_in(streams_of[4], 71), 0),
        "coarse_duals": bell_draw(streams_of[2], (PROTO_BLOCKS, BLOCK_COLS), 2.0, 8.0, ((0, 32),), jnp.float32),
        "active": draw_active(jax.random.fold_in(streams_of[4], 71), 0),
    }


def reference(points, prototypes, coarse_duals, active):
    def point_pass(carried):
        block_rows, targets = carried
        chosen = prototypes[targets].reshape(ACTIVE * BLOCK_COLS, D)
        scores = jnp.dot(block_rows, chosen.T, preferred_element_type=jnp.float32)
        shifted = scores + coarse_duals[targets].reshape(ACTIVE * BLOCK_COLS)[None, :]
        peak = jnp.max(shifted, axis=1)
        duals = -(peak + jnp.log(jnp.sum(jnp.exp(shifted - peak[:, None]), axis=1)))
        column_arg = scores + duals[:, None]
        col_peak = jnp.max(column_arg, axis=0)
        col_mass = jnp.sum(jnp.exp(column_arg - col_peak[None, :]), axis=0)
        return duals, col_peak.reshape(ACTIVE, BLOCK_COLS), col_mass.reshape(ACTIVE, BLOCK_COLS)

    point_duals, col_peak, col_mass = lax.map(point_pass, (points, active))
    flat_blocks = active.reshape(-1)
    peaks = col_peak.reshape(-1, BLOCK_COLS)
    masses = col_mass.reshape(-1, BLOCK_COLS)
    block_peak = jnp.full((PROTO_BLOCKS, BLOCK_COLS), -jnp.inf, dtype=jnp.float32).at[flat_blocks].max(peaks)
    scaled = masses * jnp.exp(peaks - block_peak[flat_blocks])
    block_mass = jnp.zeros((PROTO_BLOCKS, BLOCK_COLS), dtype=jnp.float32).at[flat_blocks].add(scaled)
    new_duals = -(block_peak + jnp.log(block_mass))
    return point_duals, new_duals
```

```python
import functools

import jax
import jax.numpy as jnp
from jax import lax
from jax.experimental import pallas as pl
from jax.experimental.pallas import tpu as pltpu
from jax.sharding import Mesh, PartitionSpec as P

LOWEST = -1e30
PLANE = 4


def scores_of(points_ref, protos_ref, k, first, second):
    rows = jnp.concatenate([points_ref[first], points_ref[second]], axis=0)
    return lax.dot_general(
        protos_ref[k], rows, (((1,), (1,)), ((), ())), preferred_element_type=jnp.float32
    )


def row_kernel(order_ref, count_ref, points_ref, protos_ref, coarse_ref, out_ref):
    depth, most, rows = out_ref.shape
    out_ref[...] = jnp.full(out_ref.shape, LOWEST, jnp.float32)
    for k in range(depth):
        count = count_ref[k]

        def step(s, _):
            first = order_ref[k, 2 * s]
            second = order_ref[k, 2 * s + 1]
            shifted = scores_of(points_ref, protos_ref, k, first, second) + coarse_ref[k]
            peak = jnp.max(shifted, axis=0, keepdims=True)
            mass = jnp.sum(jnp.exp(shifted - peak), axis=0, keepdims=True)
            value = peak + jnp.log(mass)
            spare = jnp.where(2 * s + 1 < count, second, most - 1)
            out_ref[k, pl.ds(first, 1)] = value[:, :rows]
            out_ref[k, pl.ds(spare, 1)] = value[:, rows:]
            return 0

        lax.fori_loop(0, (count + 1) // 2, step, 0)


def column_kernel(order_ref, count_ref, points_ref, protos_ref, duals_ref, out_ref, peak_ref, mass_ref):
    depth = out_ref.shape[0]
    for k in range(depth):
        count = count_ref[k]
        peak_ref[...] = jnp.full(peak_ref.shape, LOWEST, jnp.float32)
        mass_ref[...] = jnp.zeros(mass_ref.shape, jnp.float32)

        def step(s, _):
            first = order_ref[k, 2 * s]
            second = order_ref[k, 2 * s + 1]
            scores = scores_of(points_ref, protos_ref, k, first, second)
            after = duals_ref[pl.ds(second, 1)] + jnp.where(2 * s + 1 < count, 0.0, LOWEST)
            arg = scores + jnp.concatenate([duals_ref[pl.ds(first, 1)], after], axis=1)
            old = peak_ref[...]
            new = jnp.maximum(old, arg)
            mass_ref[...] = mass_ref[...] * jnp.exp(old - new) + jnp.exp(arg - new)
            peak_ref[...] = new
            return 0

        lax.fori_loop(0, (count + 1) // 2, step, 0)
        peak = jnp.max(peak_ref[...], axis=1, keepdims=True)
        mass = jnp.sum(mass_ref[...] * jnp.exp(peak_ref[...] - peak), axis=1, keepdims=True)
        value = jnp.where(mass > 0.0, peak + jnp.log(mass), LOWEST)
        out_ref[k] = value.reshape(1, -1)


def lse(x, axis):
    peak = jnp.max(x, axis=axis, keepdims=True)
    return jnp.squeeze(peak + jnp.log(jnp.sum(jnp.exp(x - peak), axis=axis, keepdims=True)), axis)


def body(points, prototypes, coarse_duals, active):
    depth = lax.axis_size("z")
    owners = lax.axis_size("proto")
    plane = lax.axis_size("r")
    blocks, rows, _ = points.shape
    columns = prototypes.shape[1]
    held = blocks * plane

    protos = lax.all_gather(prototypes, "z", axis=0, tiled=True)
    coarse = lax.all_gather(coarse_duals, "z", axis=0, tiled=True)
    wide = lax.all_gather(points, "proto", axis=2, tiled=True)
    wide = lax.all_gather(wide, "r", axis=0, tiled=True)
    targets = lax.all_gather(active, "r", axis=0, tiled=True)

    mine = (jnp.arange(depth, dtype=jnp.int32) * plane + lax.axis_index("r")) * owners + lax.axis_index("proto")
    named = jnp.any(targets[None] == mine[:, None, None], axis=2)
    ids = jnp.arange(held, dtype=jnp.int32)
    place = jnp.sum((named[:, None, :] & (ids[None, :] < ids[:, None])[None]).astype(jnp.int32), axis=2)
    hit = named[:, None, :] & (place[:, None, :] == ids[None, :, None])
    order = jnp.sum(jnp.where(hit, ids[None, None, :], 0), axis=2)
    count = jnp.sum(named.astype(jnp.int32), axis=1)

    smem = pl.BlockSpec(memory_space=pltpu.SMEM)
    vmem = pl.BlockSpec(memory_space=pltpu.VMEM)
    params = pltpu.CompilerParams(vmem_limit_bytes=56 * 1024 * 1024)
    partial = pl.pallas_call(
        row_kernel,
        out_shape=jax.ShapeDtypeStruct((depth, held + 8, rows), jnp.float32),
        in_specs=[smem, smem, vmem, vmem, vmem],
        out_specs=vmem,
        compiler_params=params,
    )(order, count, wide, protos, coarse[:, :, None])
    partial = lse(partial[:, :held], 0)
    partial = lax.all_gather(partial[None], ("r", "proto"), axis=0, tiled=True)
    duals = -lse(partial, 0)
    point_duals = lax.dynamic_slice_in_dim(duals, lax.axis_index("r") * blocks, blocks, 0)
    sums = pl.pallas_call(
        column_kernel,
        out_shape=jax.ShapeDtypeStruct((depth, 1, columns), jnp.float32),
        in_specs=[smem, smem, vmem, vmem, vmem],
        out_specs=vmem,
        scratch_shapes=[
            pltpu.VMEM((columns, 2 * rows), jnp.float32),
            pltpu.VMEM((columns, 2 * rows), jnp.float32),
        ],
        compiler_params=params,
    )(order, count, wide, protos, duals)
    sums = lax.all_to_all(sums[:, 0], "z", split_axis=0, concat_axis=0, tiled=True)
    return point_duals, -lse(sums, 0)[None]


def solution(mesh):
    groups, owners = mesh.shape["pts"], mesh.shape["proto"]
    plane = PLANE if groups % PLANE == 0 else 1
    grid = Mesh(mesh.devices.reshape(groups // plane, plane, owners), ("z", "r", "proto"))
    pts = ("z", "r")
    both = ("z", "r", "proto")
    return jax.shard_map(
        body,
        mesh=grid,
        in_specs=(P(pts, None, "proto"), P(both, None, None), P(both, None), P(pts, None)),
        out_specs=(P(pts, None), P(both, None)),
        check_vma=False,
    )
```

```python
import functools

import jax
import jax.numpy as jnp
from jax import lax
from jax.experimental import pallas as pl
from jax.experimental.pallas import tpu as pltpu
from jax.sharding import Mesh, PartitionSpec as P

LOWEST = -1e30
PLANE = 4
MESH = pl.DeviceIdType.MESH


def block_of(points_ref, i):
    _, owners, blocks, _, _ = points_ref.shape
    return jnp.concatenate([points_ref[i // blocks, o, i % blocks] for o in range(owners)], axis=1)


def scores_of(points_ref, protos_ref, k, first, second):
    rows = jnp.concatenate([block_of(points_ref, first), block_of(points_ref, second)], axis=0)
    return lax.dot_general(
        protos_ref[k], rows, (((1,), (1,)), ((), ())), preferred_element_type=jnp.float32
    )


def row_kernel(order_ref, count_ref, points_ref, protos_ref, coarse_ref, out_ref):
    depth, most, rows = out_ref.shape
    out_ref[...] = jnp.full(out_ref.shape, LOWEST, jnp.float32)
    for k in range(depth):
        count = count_ref[k]
        coarse = coarse_ref[k].reshape(-1, 1)

        def step(s, _):
            first = order_ref[k, 2 * s]
            second = order_ref[k, 2 * s + 1]
            shifted = scores_of(points_ref, protos_ref, k, first, second) + coarse
            peak = jnp.max(shifted, axis=0, keepdims=True)
            mass = jnp.sum(jnp.exp(shifted - peak), axis=0, keepdims=True)
            value = peak + jnp.log(mass)
            spare = jnp.where(2 * s + 1 < count, second, most - 1)
            out_ref[k, pl.ds(first, 1)] = value[:, :rows]
            out_ref[k, pl.ds(spare, 1)] = value[:, rows:]
            return 0

        lax.fori_loop(0, (count + 1) // 2, step, 0)


def column_kernel(order_ref, count_ref, points_ref, protos_ref, duals_ref, out_ref, peak_ref, mass_ref):
    depth = out_ref.shape[0]
    for k in range(depth):
        count = count_ref[k]
        peak_ref[...] = jnp.full(peak_ref.shape, LOWEST, jnp.float32)
        mass_ref[...] = jnp.zeros(mass_ref.shape, jnp.float32)

        def step(s, _):
            first = order_ref[k, 2 * s]
            second = order_ref[k, 2 * s + 1]
            scores = scores_of(points_ref, protos_ref, k, first, second)
            after = duals_ref[pl.ds(second, 1)] + jnp.where(2 * s + 1 < count, 0.0, LOWEST)
            arg = scores + jnp.concatenate([duals_ref[pl.ds(first, 1)], after], axis=1)
            old = peak_ref[...]
            new = jnp.maximum(old, arg)
            mass_ref[...] = mass_ref[...] * jnp.exp(old - new) + jnp.exp(arg - new)
            peak_ref[...] = new
            return 0

        lax.fori_loop(0, (count + 1) // 2, step, 0)
        peak = jnp.max(peak_ref[...], axis=1, keepdims=True)
        mass = jnp.sum(mass_ref[...] * jnp.exp(peak_ref[...] - peak), axis=1, keepdims=True)
        value = jnp.where(mass > 0.0, peak + jnp.log(mass), LOWEST)
        out_ref[k] = value.reshape(1, -1)


def lse(x, axis):
    peak = jnp.max(x, axis=axis, keepdims=True)
    return jnp.squeeze(peak + jnp.log(jnp.sum(jnp.exp(x - peak), axis=axis, keepdims=True)), axis)


def place(z, r, o):
    return {"z": z, "r": r, "proto": o}


def greet(partners, count):
    barrier = pltpu.get_barrier_semaphore()
    for where, there in partners:
        if where is None:
            pl.semaphore_signal(barrier, inc=1, device_id=there, device_id_type=MESH)
        else:

            @pl.when(where)
            def _():
                pl.semaphore_signal(barrier, inc=1, device_id=there, device_id_type=MESH)

    pl.semaphore_wait(barrier, count)


def gather_kernel(
    sizes,
    points_ref,
    protos_ref,
    coarse_ref,
    active_ref,
    wide_ref,
    blocks_ref,
    duals_ref,
    targets_ref,
    local_sem,
    up_send,
    up_recv,
    down_send,
    down_recv,
    point_send,
    point_recv,
    hop_send,
    hop_recv,
):
    depth, plane, owners = sizes
    halves = 2 if plane % 2 == 0 else 1
    wings = plane // halves
    z, r, o = lax.axis_index("z"), lax.axis_index("r"), lax.axis_index("proto")
    a, c = r // halves, r % halves

    def shifted(da, do):
        return lax.rem(a + da + wings, wings) * halves, lax.rem(o + do + owners, owners)

    moves = [(da, do) for da in range(wings) for do in range(owners) if da or do]
    moves.sort(key=lambda m: (m[0] > 0 and m[1] > 0, m[0] > 0))
    twin = place(z, a * halves + (1 - c), o)
    partners = [(z + 1 < depth, place(z + 1, r, o)), (z > 0, place(z - 1, r, o))]
    for da, do in moves:
        base, there = shifted(da, do)
        partners.append((None, place(z, base + c, there)))
    if halves == 2:
        partners.append((None, twin))
    greet(partners, len(partners) - 2 + (z + 1 < depth).astype(jnp.int32) + (z > 0).astype(jnp.int32))

    def chain(t, up):
        slot = z - t if up else z + t
        send, recv = (up_send, up_recv) if up else (down_send, down_recv)
        there = place(z + 1 if up else z - 1, r, o)
        return [
            pltpu.make_async_remote_copy(
                src_ref=own if t == 0 else whole.at[pl.ds(slot, 1)],
                dst_ref=whole.at[pl.ds(slot, 1)],
                send_sem=send.at[t, n],
                recv_sem=recv.at[t, n],
                device_id=there,
                device_id_type=MESH,
            )
            for n, (own, whole) in enumerate([(protos_ref, blocks_ref), (coarse_ref, duals_ref)])
        ]

    def arriving(t, up):
        slot = z - 1 - t if up else z + 1 + t
        recv = up_recv if up else down_recv
        return [
            pltpu.make_async_remote_copy(
                src_ref=whole.at[pl.ds(slot, 1)],
                dst_ref=whole.at[pl.ds(slot, 1)],
                send_sem=recv.at[t, n],
                recv_sem=recv.at[t, n],
                device_id=place(z, r, o),
                device_id_type=MESH,
            )
            for n, whole in enumerate([blocks_ref, duals_ref])
        ]

    def sends(t, up):
        return (z - t >= 0) & (z + 1 < depth) if up else (z + t < depth) & (z > 0)

    def receives(t, up):
        return z - 1 - t >= 0 if up else z + 1 + t < depth

    def start_chain(t):
        for up in (True, False):

            @pl.when(sends(t, up))
            def _():
                for copy in chain(t, up):
                    copy.start()

    def wait_chain(t):
        for up in (True, False):

            @pl.when(receives(t, up))
            def _():
                for copy in arriving(t, up):
                    copy.wait_recv()

    def pair(own, sr, so, there, send, recv, n, tags):
        copies = [
            pltpu.make_async_remote_copy(
                src_ref=points_ref if own else wide_ref.at[sr, so],
                dst_ref=wide_ref.at[sr, so],
                send_sem=send.at[n, 0],
                recv_sem=recv.at[n, 0],
                device_id=there,
                device_id_type=MESH,
            )
        ]
        if tags:
            copies.append(
                pltpu.make_async_remote_copy(
                    src_ref=active_ref if own else targets_ref.at[sr],
                    dst_ref=targets_ref.at[sr],
                    send_sem=send.at[n, 1],
                    recv_sem=recv.at[n, 1],
                    device_id=there,
                    device_id_type=MESH,
                )
            )
        return copies

    local = [
        pltpu.make_async_copy(protos_ref, blocks_ref.at[pl.ds(z, 1)], local_sem.at[0]),
        pltpu.make_async_copy(coarse_ref, duals_ref.at[pl.ds(z, 1)], local_sem.at[1]),
        pltpu.make_async_copy(points_ref, wide_ref.at[r, o], local_sem.at[2]),
        pltpu.make_async_copy(active_ref, targets_ref.at[r], local_sem.at[3]),
    ]
    start_chain(0)
    outgoing = []
    for n, (da, do) in enumerate(moves):
        base, there = shifted(da, do)
        copies = pair(True, r, o, place(z, base + c, there), point_send, point_recv, n, do == 0)
        for copy in copies:
            copy.start()
        outgoing += copies
    spare = len(moves)
    if halves == 2:
        copies = pair(True, r, o, twin, hop_send, hop_recv, spare, True)
        for copy in copies:
            copy.start()
        outgoing += copies
    for copy in local:
        copy.start()

    def pass_on(n):
        da, do = moves[n]
        base, from_o = shifted(-da, -do)
        copies = pair(False, base + c, from_o, twin, point_send, point_recv, n, do == 0)
        for copy in copies:
            copy.wait_recv()
        if halves == 2:
            copies = pair(False, base + c, from_o, twin, hop_send, hop_recv, n, do == 0)
            for copy in copies:
                copy.start()
            outgoing.extend(copies)

    steps = max(depth - 1, 1)
    share = -(-len(moves) // steps)
    done = 0
    for t in range(steps):
        if t < depth - 1:
            wait_chain(t)
            if t + 1 < depth - 1:
                start_chain(t + 1)
        for n in range(done, min(done + share, len(moves))):
            pass_on(n)
        done = min(done + share, len(moves))
    if halves == 2:
        for n, (da, do) in enumerate(moves + [(0, 0)]):
            base, from_o = shifted(-da, -do)
            for copy in pair(False, base + 1 - c, from_o, twin, hop_send, hop_recv, n, do == 0):
                copy.wait_recv()
    for copy in outgoing:
        copy.wait_send()
    for t in range(depth - 1):
        for up in (True, False):

            @pl.when(sends(t, up))
            def _():
                for copy in chain(t, up):
                    copy.wait_send()

    for copy in local:
        copy.wait()


def plane_kernel(sizes, part_ref, out_ref, all_ref, send_sem, recv_sem):
    depth, plane, owners = sizes
    z, r, o = lax.axis_index("z"), lax.axis_index("r"), lax.axis_index("proto")
    me = r * owners + o
    held = part_ref.shape[1]
    moves = [(dr, do) for dr in range(plane) for do in range(owners) if dr or do]

    def spot(dr, do):
        return lax.rem(r + dr + plane, plane), lax.rem(o + do + owners, owners)

    greet([(None, place(z, *spot(*move))) for move in moves], len(moves))
    all_ref[me] = lse(part_ref[...], 0)
    copies = [
        pltpu.make_async_remote_copy(
            src_ref=all_ref.at[me],
            dst_ref=all_ref.at[me],
            send_sem=send_sem.at[n],
            recv_sem=recv_sem.at[n],
            device_id=place(z, *spot(*move)),
            device_id_type=MESH,
        )
        for n, move in enumerate(moves)
    ]
    for copy in copies:
        copy.start()
    for n, (dr, do) in enumerate(moves):
        sr, so = spot(-dr, -do)
        slot = all_ref.at[sr * owners + so]
        pltpu.make_async_remote_copy(
            src_ref=slot,
            dst_ref=slot,
            send_sem=send_sem.at[n],
            recv_sem=recv_sem.at[n],
            device_id=place(z, sr, so),
            device_id_type=MESH,
        ).wait_recv()
    out_ref[...] = -lse(all_ref[...], 0)
    for copy in copies:
        copy.wait_send()


def line_kernel(sizes, part_ref, out_ref, all_ref, send_sem, recv_sem):
    depth, plane, owners = sizes
    z, r, o = lax.axis_index("z"), lax.axis_index("r"), lax.axis_index("proto")
    greet([(None, place(lax.rem(z + d, depth), r, o)) for d in range(1, depth)], depth - 1)
    all_ref[z] = part_ref[z]
    copies = []
    for d in range(1, depth):
        there = lax.rem(z + d, depth)
        copies.append(
            pltpu.make_async_remote_copy(
                src_ref=part_ref.at[there],
                dst_ref=all_ref.at[z],
                send_sem=send_sem.at[d],
                recv_sem=recv_sem.at[d],
                device_id=place(there, r, o),
                device_id_type=MESH,
            )
        )
    for copy in copies:
        copy.start()
    for d in range(1, depth):
        slot = all_ref.at[lax.rem(z + depth - d, depth)]
        pltpu.make_async_remote_copy(
            src_ref=slot,
            dst_ref=slot,
            send_sem=send_sem.at[d],
            recv_sem=recv_sem.at[d],
            device_id=place(lax.rem(z + depth - d, depth), r, o),
            device_id_type=MESH,
        ).wait_recv()
    out_ref[...] = -lse(all_ref[...], 0)
    for copy in copies:
        copy.wait_send()


def body(points, prototypes, coarse_duals, active):
    depth = lax.axis_size("z")
    owners = lax.axis_size("proto")
    plane = lax.axis_size("r")
    sizes = (depth, plane, owners)
    blocks, rows, width = points.shape
    columns, features = prototypes.shape[1:]
    held = blocks * plane
    smem = pl.BlockSpec(memory_space=pltpu.SMEM)
    vmem = pl.BlockSpec(memory_space=pltpu.VMEM)
    anywhere = pl.BlockSpec(memory_space=pl.ANY)

    dma = pltpu.SemaphoreType.DMA
    hops = plane * owners
    wide, protos, coarse, targets = pl.pallas_call(
        functools.partial(gather_kernel, sizes),
        out_shape=(
            jax.ShapeDtypeStruct((plane, owners, blocks, rows, width), points.dtype),
            jax.ShapeDtypeStruct((depth, columns, features), prototypes.dtype),
            jax.ShapeDtypeStruct((depth, 1, columns), jnp.float32),
            jax.ShapeDtypeStruct((plane,) + active.shape, active.dtype),
        ),
        in_specs=[anywhere] * 4,
        out_specs=(anywhere,) * 4,
        scratch_shapes=[dma((4,))] + [dma((depth, 2))] * 4 + [dma((hops, 2))] * 4,
        compiler_params=pltpu.CompilerParams(collective_id=0, has_side_effects=True),
    )(points, prototypes, coarse_duals[None], active)
    targets = targets.reshape(held, active.shape[1])

    mine = (jnp.arange(depth, dtype=jnp.int32) * plane + lax.axis_index("r")) * owners + lax.axis_index("proto")
    named = jnp.any(targets[None] == mine[:, None, None], axis=2)
    ids = jnp.arange(held, dtype=jnp.int32)
    spot = jnp.sum((named[:, None, :] & (ids[None, :] < ids[:, None])[None]).astype(jnp.int32), axis=2)
    hit = named[:, None, :] & (spot[:, None, :] == ids[None, :, None])
    order = jnp.sum(jnp.where(hit, ids[None, None, :], 0), axis=2)
    count = jnp.sum(named.astype(jnp.int32), axis=1)

    params = pltpu.CompilerParams(vmem_limit_bytes=56 * 1024 * 1024)
    partial = pl.pallas_call(
        row_kernel,
        out_shape=jax.ShapeDtypeStruct((depth, held + 8, rows), jnp.float32),
        in_specs=[smem, smem, vmem, vmem, vmem],
        out_specs=vmem,
        compiler_params=params,
    )(order, count, wide, protos, coarse)
    duals = pl.pallas_call(
        functools.partial(plane_kernel, sizes),
        out_shape=jax.ShapeDtypeStruct((held + 8, rows), jnp.float32),
        in_specs=[vmem],
        out_specs=vmem,
        scratch_shapes=[pltpu.VMEM((hops, held + 8, rows), jnp.float32), dma((hops,)), dma((hops,))],
        compiler_params=pltpu.CompilerParams(collective_id=1, has_side_effects=True),
    )(partial)
    point_duals = lax.dynamic_slice_in_dim(duals, lax.axis_index("r") * blocks, blocks, 0)
    sums = pl.pallas_call(
        column_kernel,
        out_shape=jax.ShapeDtypeStruct((depth, 1, columns), jnp.float32),
        in_specs=[smem, smem, vmem, vmem, vmem],
        out_specs=vmem,
        scratch_shapes=[
            pltpu.VMEM((columns, 2 * rows), jnp.float32),
            pltpu.VMEM((columns, 2 * rows), jnp.float32),
        ],
        compiler_params=params,
    )(order, count, wide, protos, duals)
    new_duals = pl.pallas_call(
        functools.partial(line_kernel, sizes),
        out_shape=jax.ShapeDtypeStruct((1, columns), jnp.float32),
        in_specs=[vmem],
        out_specs=vmem,
        scratch_shapes=[pltpu.VMEM((depth, 1, columns), jnp.float32), dma((depth,)), dma((depth,))],
        compiler_params=pltpu.CompilerParams(collective_id=2, has_side_effects=True),
    )(sums)
    return point_duals, new_duals


def solution(mesh):
    groups, owners = mesh.shape["pts"], mesh.shape["proto"]
    plane = PLANE if groups % PLANE == 0 else 1
    grid = Mesh(mesh.devices.reshape(groups // plane, plane, owners), ("z", "r", "proto"))
    pts = ("z", "r")
    both = ("z", "r", "proto")
    return jax.shard_map(
        body,
        mesh=grid,
        in_specs=(P(pts, None, "proto"), P(both, None, None), P(both, None), P(pts, None)),
        out_specs=(P(pts, None), P(both, None)),
        check_vma=False,
    )
```

```python
import functools

import jax
import jax.numpy as jnp
from jax import lax
from jax.experimental import pallas as pl
from jax.experimental.pallas import tpu as pltpu
from jax.sharding import Mesh, PartitionSpec as P

LOWEST = -1e30
PLANE = 4
PIECES = 2
KEPT_MOST = 32 * 1024 * 1024
VMEM_MOST = 60 * 1024 * 1024
MESH = pl.DeviceIdType.MESH


def block_of(points_ref, i):
    _, owners, blocks, _, _ = points_ref.shape
    return jnp.concatenate([points_ref[i // blocks, o, i % blocks] for o in range(owners)], axis=1)


def scores_of(points_ref, protos_ref, k, s):
    rows = jnp.concatenate([block_of(points_ref, 2 * s), block_of(points_ref, 2 * s + 1)], axis=0)
    return lax.dot_general(
        protos_ref[k], rows, (((1,), (1,)), ((), ())), preferred_element_type=jnp.float32
    )


def beside(ref, s):
    return jnp.concatenate([ref[pl.ds(2 * s, 1)], ref[pl.ds(2 * s + 1, 1)]], axis=1)


def lse(x, axis):
    peak = jnp.max(x, axis=axis, keepdims=True)
    return jnp.squeeze(peak + jnp.log(jnp.sum(jnp.exp(x - peak), axis=axis, keepdims=True)), axis)


def place(z, r, o):
    return {"z": z, "r": r, "proto": o}


def greet(partners):
    barrier = pltpu.get_barrier_semaphore()
    for there in partners:
        pl.semaphore_signal(barrier, inc=1, device_id=there, device_id_type=MESH)
    pl.semaphore_wait(barrier, len(partners))


def fused_kernel(
    sizes,
    keep,
    points_ref,
    protos_ref,
    coarse_ref,
    active_ref,
    point_out,
    proto_out,
    wide_ref,
    blocks_ref,
    duals_ref,
    targets_ref,
    scores_ref,
    part_ref,
    all_ref,
    bias_ref,
    column_ref,
    line_ref,
    total_ref,
    work_ref,
    local_sem,
    up_send,
    up_recv,
    down_send,
    down_recv,
    point_send,
    point_recv,
    hop_send,
    hop_recv,
    plane_send,
    plane_recv,
    line_send,
    line_recv,
):
    depth, plane, owners = sizes
    halves = 2 if plane % 2 == 0 else 1
    wings = plane // halves
    z, r, o = lax.axis_index("z"), lax.axis_index("r"), lax.axis_index("proto")
    a, c = r // halves, r % halves

    def shifted(da, do):
        return lax.rem(a + da + wings, wings) * halves, lax.rem(o + do + owners, owners)

    moves = [(da, do) for da in range(wings) for do in range(owners) if da or do]
    moves.sort(key=lambda m: (m[0] > 0 and m[1] > 0, m[0] > 0))
    twin = place(z, a * halves + (1 - c), o)
    around = [(dr, do) for dr in range(plane) for do in range(owners) if dr or do]

    def spot(dr, do):
        return lax.rem(r + dr + plane, plane), lax.rem(o + do + owners, owners)

    partners = [place(z, *spot(*move)) for move in around]
    partners += [place(lax.rem(z + d, depth), r, o) for d in range(1, depth)]
    greet(partners)

    piece = blocks_ref.shape[1] // PIECES

    def parts(slot, n):
        cut = pl.ds(n * piece, piece)
        pairs = [(protos_ref.at[:, cut], blocks_ref.at[pl.ds(slot, 1), cut])]
        if n == 0:
            pairs.append((coarse_ref, duals_ref.at[pl.ds(slot, 1)]))
        return pairs

    def chain(t, up, n):
        slot = z - t if up else z + t
        send, recv = (up_send, up_recv) if up else (down_send, down_recv)
        return [
            pltpu.make_async_remote_copy(
                src_ref=own if t == 0 else whole,
                dst_ref=whole,
                send_sem=send.at[t, n + PIECES * m],
                recv_sem=recv.at[t, n + PIECES * m],
                device_id=place(z + 1 if up else z - 1, r, o),
                device_id_type=MESH,
            )
            for m, (own, whole) in enumerate(parts(slot, n))
        ]

    def arriving(t, up, n):
        slot = z - 1 - t if up else z + 1 + t
        recv = up_recv if up else down_recv
        return [
            pltpu.make_async_remote_copy(
                src_ref=whole,
                dst_ref=whole,
                send_sem=recv.at[t, n + PIECES * m],
                recv_sem=recv.at[t, n + PIECES * m],
                device_id=place(z, r, o),
                device_id_type=MESH,
            )
            for m, (_, whole) in enumerate(parts(slot, n))
        ]

    def sends(t, up):
        return (z - t >= 0) & (z + 1 < depth) if up else (z + t < depth) & (z > 0)

    def receives(t, up):
        return z - 1 - t >= 0 if up else z + 1 + t < depth

    def start_chain(t, n):
        for up in (True, False):

            @pl.when(sends(t, up))
            def _():
                for copy in chain(t, up, n):
                    copy.start()

    def wait_chain(t, n):
        for up in (True, False):

            @pl.when(receives(t, up))
            def _():
                for copy in arriving(t, up, n):
                    copy.wait_recv()

    def pair(own, sr, so, there, send, recv, n, tags):
        copies = [
            pltpu.make_async_remote_copy(
                src_ref=points_ref if own else wide_ref.at[sr, so],
                dst_ref=wide_ref.at[sr, so],
                send_sem=send.at[n, 0],
                recv_sem=recv.at[n, 0],
                device_id=there,
                device_id_type=MESH,
            )
        ]
        if tags:
            copies.append(
                pltpu.make_async_remote_copy(
                    src_ref=active_ref if own else targets_ref.at[sr],
                    dst_ref=targets_ref.at[sr],
                    send_sem=send.at[n, 1],
                    recv_sem=recv.at[n, 1],
                    device_id=there,
                    device_id_type=MESH,
                )
            )
        return copies

    local = [
        pltpu.make_async_copy(protos_ref, blocks_ref.at[pl.ds(z, 1)], local_sem.at[0]),
        pltpu.make_async_copy(coarse_ref, duals_ref.at[pl.ds(z, 1)], local_sem.at[1]),
        pltpu.make_async_copy(points_ref, wide_ref.at[r, o], local_sem.at[2]),
        pltpu.make_async_copy(active_ref, targets_ref.at[r], local_sem.at[3]),
    ]
    for n in range(PIECES):
        start_chain(0, n)
    outgoing = []
    for n, (da, do) in enumerate(moves):
        base, there = shifted(da, do)
        copies = pair(True, r, o, place(z, base + c, there), point_send, point_recv, n, do == 0)
        for copy in copies:
            copy.start()
        outgoing += copies
    spare = len(moves)
    if halves == 2:
        copies = pair(True, r, o, twin, hop_send, hop_recv, spare, True)
        for copy in copies:
            copy.start()
        outgoing += copies
    for copy in local:
        copy.start()

    def pass_on(n):
        da, do = moves[n]
        base, from_o = shifted(-da, -do)
        copies = pair(False, base + c, from_o, twin, point_send, point_recv, n, do == 0)
        for copy in copies:
            copy.wait_recv()
        if halves == 2:
            copies = pair(False, base + c, from_o, twin, hop_send, hop_recv, n, do == 0)
            for copy in copies:
                copy.start()
            outgoing.extend(copies)

    def settle_points():
        for n in range(len(moves)):
            pass_on(n)
        if halves == 2:
            for n, (da, do) in enumerate(moves + [(0, 0)]):
                base, from_o = shifted(-da, -do)
                for copy in pair(False, base + 1 - c, from_o, twin, hop_send, hop_recv, n, do == 0):
                    copy.wait_recv()
        for copy in local:
            copy.wait()

    held, rows = all_ref.shape[1:]
    columns = blocks_ref.shape[1]
    doubles = held // 2

    def named(k):
        block = (k * plane + r) * owners + o
        tags = targets_ref[...].reshape(held, targets_ref.shape[2])
        return jnp.max(jnp.where(tags == block, 1.0, 0.0), axis=1, keepdims=True) > 0.0

    def score(k):
        coarse = duals_ref[k].reshape(-1, 1)

        def step(s, _):
            found = scores_of(wide_ref, blocks_ref, k, s)
            if keep:
                scores_ref[k, s] = found
            given = found + coarse
            peak = jnp.max(given, axis=0, keepdims=True)
            value = peak + jnp.log(jnp.sum(jnp.exp(given - peak), axis=0, keepdims=True))
            part_ref[k, pl.ds(2 * s, 1)] = value[:, :rows]
            part_ref[k, pl.ds(2 * s + 1, 1)] = value[:, rows:]
            return 0

        lax.fori_loop(0, doubles, step, 0)
        part_ref[k] = jnp.where(named(k), part_ref[k], LOWEST)

    def score_step(t):
        if t < 0:
            score(z)
            return

        def side(n, _):
            slot = z + (1 + t) * (2 * n - 1)

            @pl.when((slot >= 0) & (slot < depth))
            def _():
                score(slot)

            return 0

        lax.fori_loop(0, 2, side, 0)

    todo = list(range(-1, depth - 1))
    settled = False
    for t in range(depth - 1):
        for n in range(PIECES):
            wait_chain(t, n)
            if t + 1 < depth - 1:
                start_chain(t + 1, n)
            if t >= min(1, depth - 2):
                if not settled:
                    settle_points()
                    settled = True
                limit = t - 1 if n < PIECES - 1 else t
                if todo and todo[0] <= limit:
                    score_step(todo.pop(0))
    if not settled:
        settle_points()
    for t in todo:
        score_step(t)

    me = r * owners + o
    all_ref[me] = lse(part_ref[...], 0)
    for n, move in enumerate(around):
        copy = pltpu.make_async_remote_copy(
            src_ref=all_ref.at[me],
            dst_ref=all_ref.at[me],
            send_sem=plane_send.at[n],
            recv_sem=plane_recv.at[n],
            device_id=place(z, *spot(*move)),
            device_id_type=MESH,
        )
        copy.start()
        outgoing.append(copy)
    for n, (dr, do) in enumerate(around):
        sr, so = spot(-dr, -do)
        slot = all_ref.at[sr * owners + so]
        pltpu.make_async_remote_copy(
            src_ref=slot,
            dst_ref=slot,
            send_sem=plane_send.at[n],
            recv_sem=plane_recv.at[n],
            device_id=place(z, sr, so),
            device_id_type=MESH,
        ).wait_recv()
    found = -lse(all_ref[...], 0)
    work_ref[...] = found
    count = points_ref.shape[0]
    point_out[...] = work_ref[pl.ds(pl.multiple_of(r * count, count), count)]

    strip = 64

    def column(k):
        bias_ref[...] = jnp.where(named(k), work_ref[...], LOWEST)

        def over(n, _):
            cut = pl.ds(pl.multiple_of(n * strip, strip), strip)
            peak = jnp.full((strip, 2 * rows), LOWEST, jnp.float32)
            for s in range(doubles):
                peak = jnp.maximum(peak, scores_ref[k, s, cut] + beside(bias_ref, s))
            peak = jnp.max(peak, axis=1, keepdims=True)
            mass = jnp.zeros((strip, 2 * rows), jnp.float32)
            for s in range(doubles):
                mass = mass + jnp.exp(scores_ref[k, s, cut] + beside(bias_ref, s) - peak)
            column_ref[cut] = peak + jnp.log(jnp.sum(mass, axis=1, keepdims=True))
            return 0

        def again(s, _):
            arg = scores_of(wide_ref, blocks_ref, k, s) + beside(bias_ref, s)
            old = scores_ref[0]
            new = jnp.maximum(old, arg)
            scores_ref[1] = scores_ref[1] * jnp.exp(old - new) + jnp.exp(arg - new)
            scores_ref[0] = new
            return 0

        if keep:
            lax.fori_loop(0, columns // strip, over, 0)
        else:
            scores_ref[0] = jnp.full((columns, 2 * rows), LOWEST, jnp.float32)
            scores_ref[1] = jnp.zeros((columns, 2 * rows), jnp.float32)
            lax.fori_loop(0, doubles, again, 0)
            peak = jnp.max(scores_ref[0], axis=1, keepdims=True)
            mass = jnp.sum(scores_ref[1] * jnp.exp(scores_ref[0] - peak), axis=1, keepdims=True)
            column_ref[...] = peak + jnp.log(mass)
        line_ref[k] = column_ref[...].reshape(1, -1)

    for d in range(1, depth):
        there = lax.rem(z + d, depth)
        column(there)
        copy = pltpu.make_async_remote_copy(
            src_ref=line_ref.at[there],
            dst_ref=total_ref.at[z],
            send_sem=line_send.at[d],
            recv_sem=line_recv.at[d],
            device_id=place(there, r, o),
            device_id_type=MESH,
        )
        copy.start()
        outgoing.append(copy)
    column(z)
    total_ref[z] = line_ref[z]
    for d in range(1, depth):
        source = lax.rem(z + depth - d, depth)
        slot = total_ref.at[source]
        pltpu.make_async_remote_copy(
            src_ref=slot,
            dst_ref=slot,
            send_sem=line_send.at[d],
            recv_sem=line_recv.at[d],
            device_id=place(source, r, o),
            device_id_type=MESH,
        ).wait_recv()
    proto_out[...] = -lse(total_ref[...], 0)
    for copy in outgoing:
        copy.wait_send()
    for t in range(depth - 1):
        for n in range(PIECES):
            for up in (True, False):

                @pl.when(sends(t, up))
                def _():
                    for copy in chain(t, up, n):
                        copy.wait_send()


def body(points, prototypes, coarse_duals, active):
    depth = lax.axis_size("z")
    owners = lax.axis_size("proto")
    plane = lax.axis_size("r")
    blocks, rows, width = points.shape
    columns, features = prototypes.shape[1:]
    held = blocks * plane
    hops = plane * owners
    keep = depth * held * rows * columns * 4 <= KEPT_MOST
    vmem = pl.BlockSpec(memory_space=pltpu.VMEM)
    anywhere = pl.BlockSpec(memory_space=pl.ANY)
    dma = pltpu.SemaphoreType.DMA
    real = jnp.float32
    scores = (depth, held // 2, columns, 2 * rows) if keep else (2, columns, 2 * rows)
    return pl.pallas_call(
        functools.partial(fused_kernel, (depth, plane, owners), keep),
        out_shape=(
            jax.ShapeDtypeStruct((blocks, rows), real),
            jax.ShapeDtypeStruct((1, columns), real),
        ),
        in_specs=[anywhere] * 4,
        out_specs=(vmem, vmem),
        scratch_shapes=[
            pltpu.VMEM((plane, owners, blocks, rows, width), points.dtype),
            pltpu.VMEM((depth, columns, features), prototypes.dtype),
            pltpu.VMEM((depth, 1, columns), real),
            pltpu.VMEM((plane,) + active.shape, active.dtype),
            pltpu.VMEM(scores, real),
            pltpu.VMEM((depth, held, rows), real),
            pltpu.VMEM((hops, held, rows), real),
            pltpu.VMEM((held, rows), real),
            pltpu.VMEM((columns, 1), real),
            pltpu.VMEM((depth, 1, columns), real),
            pltpu.VMEM((depth, 1, columns), real),
            pltpu.VMEM((held, rows), real),
            dma((4,)),
        ]
        + [dma((depth, 2 * PIECES))] * 4
        + [dma((hops, 2))] * 4
        + [dma((hops,))] * 2
        + [dma((depth,))] * 2,
        compiler_params=pltpu.CompilerParams(
            collective_id=0, has_side_effects=True, vmem_limit_bytes=VMEM_MOST
        ),
    )(points, prototypes, coarse_duals[None], active)


def solution(mesh):
    groups, owners = mesh.shape["pts"], mesh.shape["proto"]
    plane = PLANE if groups % PLANE == 0 else 1
    grid = Mesh(mesh.devices.reshape(groups // plane, plane, owners), ("z", "r", "proto"))
    pts = ("z", "r")
    both = ("z", "r", "proto")
    return jax.shard_map(
        body,
        mesh=grid,
        in_specs=(P(pts, None, "proto"), P(both, None, None), P(both, None), P(pts, None)),
        out_specs=(P(pts, None), P(both, None)),
        check_vma=False,
    )
```

```python
import functools

import jax
import jax.numpy as jnp
from jax import lax
from jax.experimental import pallas as pl
from jax.experimental.pallas import tpu as pltpu
from jax.sharding import Mesh, PartitionSpec as P

LOWEST = -1e30
PLANE = 4
PIECES = 2
CUTS = 1
UNROLL = 4
KEPT_MOST = 32 * 1024 * 1024
VMEM_MOST = 60 * 1024 * 1024
MESH = pl.DeviceIdType.MESH


def block_of(points_ref, i):
    _, owners, blocks, _, _ = points_ref.shape
    return jnp.concatenate([points_ref[i // blocks, o, i % blocks] for o in range(owners)], axis=1)


def scores_of(points_ref, protos_ref, k, cut, s):
    rows = jnp.concatenate([block_of(points_ref, 2 * s), block_of(points_ref, 2 * s + 1)], axis=0)
    return lax.dot_general(
        protos_ref[k, cut], rows, (((1,), (1,)), ((), ())), preferred_element_type=jnp.float32
    )


def beside(ref, s):
    return jnp.concatenate([ref[pl.ds(2 * s, 1)], ref[pl.ds(2 * s + 1, 1)]], axis=1)


def lse(x, axis):
    peak = jnp.max(x, axis=axis, keepdims=True)
    return jnp.squeeze(peak + jnp.log(jnp.sum(jnp.exp(x - peak), axis=axis, keepdims=True)), axis)


def place(z, r, o):
    return {"z": z, "r": r, "proto": o}


def greet(partners):
    barrier = pltpu.get_barrier_semaphore()
    for there in partners:
        pl.semaphore_signal(barrier, inc=1, device_id=there, device_id_type=MESH)
    pl.semaphore_wait(barrier, len(partners))


def fused_kernel(
    sizes,
    keep,
    points_ref,
    protos_ref,
    coarse_ref,
    active_ref,
    point_out,
    proto_out,
    wide_ref,
    blocks_ref,
    duals_ref,
    targets_ref,
    scores_ref,
    part_ref,
    all_ref,
    bias_ref,
    column_ref,
    line_ref,
    total_ref,
    work_ref,
    local_sem,
    up_send,
    up_recv,
    down_send,
    down_recv,
    point_send,
    point_recv,
    hop_send,
    hop_recv,
    plane_send,
    plane_recv,
    line_send,
    line_recv,
):
    depth, plane, owners = sizes
    halves = 2 if plane % 2 == 0 else 1
    wings = plane // halves
    z, r, o = lax.axis_index("z"), lax.axis_index("r"), lax.axis_index("proto")
    a, c = r // halves, r % halves

    def shifted(da, do):
        return lax.rem(a + da + wings, wings) * halves, lax.rem(o + do + owners, owners)

    moves = [(da, do) for da in range(wings) for do in range(owners) if da or do]
    moves.sort(key=lambda m: (m[0] > 0 and m[1] > 0, m[0] > 0))
    square = wings == 2 and owners == 2
    direct = [m for m in moves if not (square and m[0] and m[1])]
    half = points_ref.shape[0] // 2
    twin = place(z, a * halves + (1 - c), o)
    around = [(dr, do) for dr in range(plane) for do in range(owners) if dr or do]

    def spot(dr, do):
        return lax.rem(r + dr + plane, plane), lax.rem(o + do + owners, owners)

    partners = [place(z, *spot(*move)) for move in around]
    partners += [place(lax.rem(z + d, depth), r, o) for d in range(1, depth)]
    greet(partners)

    piece = blocks_ref.shape[1] // PIECES

    def parts(slot, n):
        cut = pl.ds(n * piece, piece)
        pairs = [(protos_ref.at[:, cut], blocks_ref.at[pl.ds(slot, 1), cut])]
        if n == 0:
            pairs.append((coarse_ref, duals_ref.at[pl.ds(slot, 1)]))
        return pairs

    def chain(t, up, n):
        slot = z - t if up else z + t
        send, recv = (up_send, up_recv) if up else (down_send, down_recv)
        return [
            pltpu.make_async_remote_copy(
                src_ref=own if t == 0 else whole,
                dst_ref=whole,
                send_sem=send.at[t, n + PIECES * m],
                recv_sem=recv.at[t, n + PIECES * m],
                device_id=place(z + 1 if up else z - 1, r, o),
                device_id_type=MESH,
            )
            for m, (own, whole) in enumerate(parts(slot, n))
        ]

    def arriving(t, up, n):
        slot = z - 1 - t if up else z + 1 + t
        recv = up_recv if up else down_recv
        return [
            pltpu.make_async_remote_copy(
                src_ref=whole,
                dst_ref=whole,
                send_sem=recv.at[t, n + PIECES * m],
                recv_sem=recv.at[t, n + PIECES * m],
                device_id=place(z, r, o),
                device_id_type=MESH,
            )
            for m, (_, whole) in enumerate(parts(slot, n))
        ]

    def sends(t, up):
        return (z - t >= 0) & (z + 1 < depth) if up else (z + t < depth) & (z > 0)

    def receives(t, up):
        return z - 1 - t >= 0 if up else z + 1 + t < depth

    def start_chain(t, n):
        for up in (True, False):

            @pl.when(sends(t, up))
            def _():
                for copy in chain(t, up, n):
                    copy.start()

    def wait_chain(t, n):
        for up in (True, False):

            @pl.when(receives(t, up))
            def _():
                for copy in arriving(t, up, n):
                    copy.wait_recv()

    def pair(own, sr, so, there, send, recv, n, tags):
        copies = [
            pltpu.make_async_remote_copy(
                src_ref=points_ref if own else wide_ref.at[sr, so],
                dst_ref=wide_ref.at[sr, so],
                send_sem=send.at[n, 0],
                recv_sem=recv.at[n, 0],
                device_id=there,
                device_id_type=MESH,
            )
        ]
        if tags:
            copies.append(
                pltpu.make_async_remote_copy(
                    src_ref=active_ref if own else targets_ref.at[sr],
                    dst_ref=targets_ref.at[sr],
                    send_sem=send.at[n, 1],
                    recv_sem=recv.at[n, 1],
                    device_id=there,
                    device_id_type=MESH,
                )
            )
        return copies

    local = [
        pltpu.make_async_copy(protos_ref, blocks_ref.at[pl.ds(z, 1)], local_sem.at[0]),
        pltpu.make_async_copy(coarse_ref, duals_ref.at[pl.ds(z, 1)], local_sem.at[1]),
        pltpu.make_async_copy(points_ref, wide_ref.at[r, o], local_sem.at[2]),
        pltpu.make_async_copy(active_ref, targets_ref.at[r], local_sem.at[3]),
    ]
    for n in range(PIECES):
        start_chain(0, n)
    outgoing = []
    for n, (da, do) in enumerate(direct):
        base, there = shifted(da, do)
        copies = pair(True, r, o, place(z, base + c, there), point_send, point_recv, n, do == 0)
        for copy in copies:
            copy.start()
        outgoing += copies
    spare = len(moves)
    if halves == 2:
        copies = pair(True, r, o, twin, hop_send, hop_recv, spare, True)
        for copy in copies:
            copy.start()
        outgoing += copies
    for copy in local:
        copy.start()

    def corner(m, da, do, target):
        base, at_o = shifted(da, do)
        slot = wide_ref.at[base + c, at_o, pl.ds(m * half, half)]
        return pltpu.make_async_remote_copy(
            src_ref=slot,
            dst_ref=slot,
            send_sem=point_send.at[len(moves) - 1 + m, 0],
            recv_sem=point_recv.at[len(moves) - 1 + m, 0],
            device_id=target,
            device_id_type=MESH,
        )

    def pass_on(n):
        da, do = moves[n]
        base, from_o = shifted(-da, -do)
        if moves[n] in direct:
            copies = pair(False, base + c, from_o, twin, point_send, point_recv, n, do == 0)
            for copy in copies:
                copy.wait_recv()
            if square:
                ahead, there = shifted(1 - da, 1 - do)
                copy = corner(do, da, do, place(z, ahead + c, there))
                copy.start()
                outgoing.append(copy)
        else:
            for m in range(2):
                corner(m, 1, 1, place(z, r, o)).wait_recv()
        if halves == 2:
            copies = pair(False, base + c, from_o, twin, hop_send, hop_recv, n, do == 0)
            for copy in copies:
                copy.start()
            outgoing.extend(copies)

    def settle_points():
        for n in range(len(moves)):
            pass_on(n)
        if halves == 2:
            for n, (da, do) in enumerate(moves + [(0, 0)]):
                base, from_o = shifted(-da, -do)
                for copy in pair(False, base + 1 - c, from_o, twin, hop_send, hop_recv, n, do == 0):
                    copy.wait_recv()
        for copy in local:
            copy.wait()

    held, rows = all_ref.shape[1:]
    columns = blocks_ref.shape[1]
    doubles = held // 2
    cut_rows = columns // CUTS

    def named(k):
        block = (k * plane + r) * owners + o
        tags = targets_ref[...].reshape(held, targets_ref.shape[2])
        return jnp.max(jnp.where(tags == block, 1.0, 0.0), axis=1, keepdims=True) > 0.0

    def score(k, n):
        coarse = duals_ref[k, :, pl.ds(n * cut_rows, cut_rows)].reshape(-1, 1)
        spots = k * CUTS + n

        def step(s, _):
            found = scores_of(wide_ref, blocks_ref, k, pl.ds(n * cut_rows, cut_rows), s)
            if keep:
                scores_ref[k, n, s] = found
            given = found + coarse
            peak = jnp.max(given, axis=0, keepdims=True)
            value = peak + jnp.log(jnp.sum(jnp.exp(given - peak), axis=0, keepdims=True))
            part_ref[spots, pl.ds(2 * s, 1)] = value[:, :rows]
            part_ref[spots, pl.ds(2 * s + 1, 1)] = value[:, rows:]
            return 0

        lax.fori_loop(0, doubles, step, 0, unroll=UNROLL)
        part_ref[spots] = jnp.where(named(k), part_ref[spots], LOWEST)

    def score_step(t, n):
        if t < 0:
            score(z, n)
            return

        def side(m, _):
            slot = z + (1 + t) * (2 * m - 1)

            @pl.when((slot >= 0) & (slot < depth))
            def _():
                score(slot, n)

            return 0

        lax.fori_loop(0, 2, side, 0)

    todo = [(t, n) for t in range(-1, depth - 1) for n in range(CUTS)]
    settled = False
    for t in range(depth - 1):
        for n in range(PIECES):
            wait_chain(t, n)
            if t + 1 < depth - 1:
                start_chain(t + 1, n)
            if t >= min(1, depth - 2):
                if not settled:
                    settle_points()
                    settled = True
                if todo and todo[0] <= (t if n == PIECES - 1 else t - 1, CUTS):
                    for _ in range(CUTS):
                        score_step(*todo.pop(0))
    if not settled:
        settle_points()
    for item in todo:
        score_step(*item)

    me = r * owners + o
    all_ref[me] = lse(part_ref[...], 0)
    for n, move in enumerate(around):
        copy = pltpu.make_async_remote_copy(
            src_ref=all_ref.at[me],
            dst_ref=all_ref.at[me],
            send_sem=plane_send.at[n],
            recv_sem=plane_recv.at[n],
            device_id=place(z, *spot(*move)),
            device_id_type=MESH,
        )
        copy.start()
        outgoing.append(copy)
    for n, (dr, do) in enumerate(around):
        sr, so = spot(-dr, -do)
        slot = all_ref.at[sr * owners + so]
        pltpu.make_async_remote_copy(
            src_ref=slot,
            dst_ref=slot,
            send_sem=plane_send.at[n],
            recv_sem=plane_recv.at[n],
            device_id=place(z, sr, so),
            device_id_type=MESH,
        ).wait_recv()
    found = -lse(all_ref[...], 0)
    work_ref[...] = found
    count = points_ref.shape[0]
    point_out[...] = work_ref[pl.ds(pl.multiple_of(r * count, count), count)]

    strip = 64

    def column(k):
        bias_ref[...] = jnp.where(named(k), work_ref[...], LOWEST)

        def over(part, n, _):
            cut = pl.ds(pl.multiple_of(n * strip, strip), strip)
            peak = jnp.full((strip, 2 * rows), LOWEST, jnp.float32)
            for s in range(doubles):
                peak = jnp.maximum(peak, scores_ref[k, part, s, cut] + beside(bias_ref, s))
            peak = jnp.max(peak, axis=1, keepdims=True)
            mass = jnp.zeros((strip, 2 * rows), jnp.float32)
            for s in range(doubles):
                mass = mass + jnp.exp(scores_ref[k, part, s, cut] + beside(bias_ref, s) - peak)
            column_ref[pl.ds(pl.multiple_of(part * cut_rows + n * strip, strip), strip)] = peak + jnp.log(jnp.sum(mass, axis=1, keepdims=True))
            return 0

        def again(s, _):
            arg = scores_of(wide_ref, blocks_ref, k, pl.ds(0, columns), s) + beside(bias_ref, s)
            old = scores_ref[0]
            new = jnp.maximum(old, arg)
            scores_ref[1] = scores_ref[1] * jnp.exp(old - new) + jnp.exp(arg - new)
            scores_ref[0] = new
            return 0

        if keep:
            for part in range(CUTS):
                lax.fori_loop(0, cut_rows // strip, functools.partial(over, part), 0)
        else:
            scores_ref[0] = jnp.full((columns, 2 * rows), LOWEST, jnp.float32)
            scores_ref[1] = jnp.zeros((columns, 2 * rows), jnp.float32)
            lax.fori_loop(0, doubles, again, 0)
            peak = jnp.max(scores_ref[0], axis=1, keepdims=True)
            mass = jnp.sum(scores_ref[1] * jnp.exp(scores_ref[0] - peak), axis=1, keepdims=True)
            column_ref[...] = peak + jnp.log(mass)
        line_ref[k] = column_ref[...].reshape(1, -1)

    for d in range(1, depth):
        there = lax.rem(z + d, depth)
        column(there)
        copy = pltpu.make_async_remote_copy(
            src_ref=line_ref.at[there],
            dst_ref=total_ref.at[z],
            send_sem=line_send.at[d],
            recv_sem=line_recv.at[d],
            device_id=place(there, r, o),
            device_id_type=MESH,
        )
        copy.start()
        outgoing.append(copy)
    column(z)
    total_ref[z] = line_ref[z]
    for d in range(1, depth):
        source = lax.rem(z + depth - d, depth)
        slot = total_ref.at[source]
        pltpu.make_async_remote_copy(
            src_ref=slot,
            dst_ref=slot,
            send_sem=line_send.at[d],
            recv_sem=line_recv.at[d],
            device_id=place(source, r, o),
            device_id_type=MESH,
        ).wait_recv()
    proto_out[...] = -lse(total_ref[...], 0)
    for copy in outgoing:
        copy.wait_send()
    for t in range(depth - 1):
        for n in range(PIECES):
            for up in (True, False):

                @pl.when(sends(t, up))
                def _():
                    for copy in chain(t, up, n):
                        copy.wait_send()


def body(points, prototypes, coarse_duals, active):
    depth = lax.axis_size("z")
    owners = lax.axis_size("proto")
    plane = lax.axis_size("r")
    blocks, rows, width = points.shape
    columns, features = prototypes.shape[1:]
    held = blocks * plane
    hops = plane * owners
    keep = depth * held * rows * columns * 4 <= KEPT_MOST
    vmem = pl.BlockSpec(memory_space=pltpu.VMEM)
    anywhere = pl.BlockSpec(memory_space=pl.ANY)
    dma = pltpu.SemaphoreType.DMA
    real = jnp.float32
    scores = (depth, CUTS, held // 2, columns // CUTS, 2 * rows) if keep else (2, columns, 2 * rows)
    return pl.pallas_call(
        functools.partial(fused_kernel, (depth, plane, owners), keep),
        out_shape=(
            jax.ShapeDtypeStruct((blocks, rows), real),
            jax.ShapeDtypeStruct((1, columns), real),
        ),
        in_specs=[anywhere] * 4,
        out_specs=(vmem, vmem),
        scratch_shapes=[
            pltpu.VMEM((plane, owners, blocks, rows, width), points.dtype),
            pltpu.VMEM((depth, columns, features), prototypes.dtype),
            pltpu.VMEM((depth, 1, columns), real),
            pltpu.VMEM((plane,) + active.shape, active.dtype),
            pltpu.VMEM(scores, real),
            pltpu.VMEM((depth * CUTS, held, rows), real),
            pltpu.VMEM((hops, held, rows), real),
            pltpu.VMEM((held, rows), real),
            pltpu.VMEM((columns, 1), real),
            pltpu.VMEM((depth, 1, columns), real),
            pltpu.VMEM((depth, 1, columns), real),
            pltpu.VMEM((held, rows), real),
            dma((4,)),
        ]
        + [dma((depth, 2 * PIECES))] * 4
        + [dma((hops, 2))] * 4
        + [dma((hops,))] * 2
        + [dma((depth,))] * 2,
        compiler_params=pltpu.CompilerParams(
            collective_id=0, has_side_effects=True, vmem_limit_bytes=VMEM_MOST
        ),
    )(points, prototypes, coarse_duals[None], active)


def solution(mesh):
    groups, owners = mesh.shape["pts"], mesh.shape["proto"]
    plane = PLANE if groups % PLANE == 0 else 1
    grid = Mesh(mesh.devices.reshape(groups // plane, plane, owners), ("z", "r", "proto"))
    pts = ("z", "r")
    both = ("z", "r", "proto")
    return jax.shard_map(
        body,
        mesh=grid,
        in_specs=(P(pts, None, "proto"), P(both, None, None), P(both, None), P(pts, None)),
        out_specs=(P(pts, None), P(both, None)),
        check_vma=False,
    )
```
